32 devices in a mesh: groups: 2 (over x), seq: 16 (over z, y, core).
Axes of the slice: x: 2, y: 2, z: 4, core: 2. Of those that a mesh axis runs over, the one named last changes fastest.
Arguments:
- tokens: bfloat16 [262144, 2048], P(('groups', 'seq')), parts along dimension 0, may hold values from -6 to 6
- right_blocks: bfloat16 [256, 512, 512], P('seq'), may hold values from -0.25 to 0.25
- left_blocks: bfloat16 [512, 256, 256], P('seq'), may hold values from -0.375 to 0.375
- chan_first: bfloat16 [32, 64, 64], replicated, may hold values from -0.75 to 0.75
- chan_second: bfloat16 [64, 32, 32], replicated, may hold values from -1 to 1
Outputs:
- mixed: bfloat16 [262144, 2048], P(('groups', 'seq')), parts along dimension 0
The draws below stay inside these ranges and needn't reach their ends.
There are 2 independent parts, one for each index of `groups`. The reference program is written for one: setup_inputs(seed, part) draws one part's arguments, and reference() takes and returns one part's arrays. A program takes and returns all parts, laid end to end along the dimension named above; an argument that names none is the same for every part. Nothing has to cross between parts.
All inputs are finite; a program needn't handle non-finite values.
Results may differ from the reference program's by a relative error of at most 0.007.
Values may be sent and summed in bfloat16 or wider, within the bound.
A program may use at most 384 MiB of HBM per device.

```python
import jax
import jax.numpy as jnp
from jax import lax

RB = 512
LB = 256
CK = 32
CM = 64
D = 2048
SEQ = 131072


def shard_levels(key, shape, shards, low, largest):
    loudness, own = 1.0, jax.random.fold_in(key, 6)
    for position, shards_of in shards:
        draws = jnp.exp(jax.random.uniform(jax.random.fold_in(own, position), (shards_of,), jnp.float32, low / len(shards), largest / len(shards)))
        loudness = loudness * jnp.repeat(draws, shape[position] // shards_of).reshape([-1 if axis == position else 1 for axis in range(len(shape))])
    return loudness


def bell_draw(stream_key, extent, deviation, bound, cuts=(), kind=jnp.bfloat16):
    level = shard_levels(stream_key, extent, cuts, -0.22, 0.18) if cuts else 1.0
    entries = jax.random.normal(stream_key, extent, jnp.float32) * deviation * level
    return jnp.minimum(jnp.maximum(entries, -bound), bound).astype(kind)


def setup_inputs(seed: int = 0, part: int = 0) -> dict:
    seeds = jax.random.split(jax.random.key(seed), 6)
    part_splits = jax.random.split(jax.random.fold_in(seeds[5], part), 6)
    tokens = bell_draw(part_splits[0], (SEQ, D), 1.0, 6.0, ((0, 16),))
    right_blocks = bell_draw(seeds[1], (LB, RB, RB), RB ** -0.5, 0.25, ((0, 16),))
    left_blocks = bell_draw(seeds[2], (RB, LB, LB), LB ** -0.5, 0.375, ((0, 16),))
    chan_first = bell_draw(seeds[3], (CK, CM, CM), CM ** -0.5, 0.75)
    chan_second = bell_draw(seeds[4], (CM, CK, CK), CK ** -0.5, 1.0)
    return dict(tokens=tokens, right_blocks=right_blocks, left_blocks=left_blocks, chan_first=chan_first, chan_second=chan_second)


def channel_mix(pair):
    block, first_w, second_w = pair
    g = block.reshape(block.shape[0], CK, CM).astype(jnp.float32)
    mid = jnp.einsum('kom,skm->sko', first_w.astype(jnp.float32), g).astype(jnp.bfloat16)
    out = jnp.einsum('mok,skm->som', second_w.astype(jnp.float32), mid.astype(jnp.float32))
    return out.reshape(block.shape[0], CK * CM).astype(jnp.bfloat16)


def reference(tokens, right_blocks, left_blocks, chan_first, chan_second):
    x = tokens.reshape(LB, RB, CK * CM)

    def right_step(pair):
        return jnp.dot(pair[0], pair[1], preferred_element_type=jnp.float32).astype(jnp.bfloat16)

    first = lax.map(right_step, (right_blocks, x))
    turned = jnp.swapaxes(first, 0, 1)
    second = lax.map(right_step, (left_blocks, turned))
    hidden = jnp.swapaxes(second, 0, 1).reshape(LB * RB, CK * CM)
    gated = (tokens.astype(jnp.float32) * hidden.astype(jnp.float32)).astype(jnp.bfloat16)
    rows_blk = 1024
    pieces = gated.reshape((LB * RB) // rows_blk, rows_blk, CK * CM)

    def mix_one(block):
        return channel_mix((block, chan_first, chan_second))

    out = lax.map(mix_one, pieces)
    return out.reshape(LB * RB, CK * CM)
```

```python
import jax
import jax.numpy as jnp
from jax import lax
from jax.experimental import pallas as pl
from jax.experimental.pallas import tpu as pltpu
from jax.sharding import PartitionSpec as P


def chunk_list(own_b):
    if own_b % 32 == 0:
        quarter = own_b // 4
        return [(0, quarter), (2 * quarter, 2 * quarter), (quarter, quarter)]
    return [(0, own_b)]


def gate_mix(tokens, hidden, mix, out, start, rows_step):
    rows_a, devices, _, width = tokens.shape
    part = hidden.shape[2]
    rows = rows_step * devices * part

    def kernel(tokens_ref, hidden_ref, mix_ref, *refs):
        out_ref = refs[-1]
        for r in range(rows_step):
            gated = tokens_ref[r].astype(jnp.float32) * hidden_ref[:, r].astype(jnp.float32)
            gated = gated.reshape(rows // rows_step, width).astype(jnp.bfloat16)
            res = jnp.dot(gated, mix_ref[...], preferred_element_type=jnp.float32)
            out_ref[r] = res.reshape(devices, part, width).astype(jnp.bfloat16)

    own = pl.BlockSpec((rows_step, devices, part, width), lambda a: (a, 0, start // part, 0))
    in_specs = [
        own,
        pl.BlockSpec((devices, rows_step, part, width), lambda a: (0, a, 0, 0)),
        pl.BlockSpec((width, width), lambda a: (0, 0)),
    ]
    operands = [tokens, hidden, mix]
    aliases = {}
    if out is not None:
        in_specs.append(pl.BlockSpec(memory_space=pl.ANY))
        operands.append(out)
        aliases = {3: 0}
    total = rows_a * devices * part
    return pl.pallas_call(
        kernel,
        grid=(rows_a // rows_step,),
        in_specs=in_specs,
        out_specs=own,
        out_shape=jax.ShapeDtypeStruct(tokens.shape, jnp.bfloat16),
        input_output_aliases=aliases,
        compiler_params=pltpu.CompilerParams(vmem_limit_bytes=56 * 2**20),
        cost_estimate=pl.CostEstimate(
            flops=2 * total * width * width,
            bytes_accessed=6 * total * width + 2 * width * width,
            transcendentals=0,
        ),
        name="gate_mix",
    )(*operands)


def plain_device(devices, tokens, right_blocks, left_blocks, chan_first, chan_second):
    rows_a, block_len, _ = right_blocks.shape
    width = tokens.shape[1]
    own_b = left_blocks.shape[0]
    blocks = left_blocks.shape[1]
    mix = (
        chan_first.transpose(0, 2, 1)[:, :, None, :].astype(jnp.float32)
        * chan_second.transpose(2, 1, 0)[:, None, :, :].astype(jnp.float32)
    ).astype(jnp.bfloat16).reshape(width, width)
    x = tokens.reshape(rows_a, block_len, width)
    right = right_blocks.reshape(rows_a, devices, own_b, block_len)
    pieces = tokens.reshape(rows_a, devices, own_b, width)
    out = None
    for start, part in chunk_list(own_b):
        first = jnp.einsum(
            "adib,abc->diac", right[:, :, start : start + part], x, preferred_element_type=jnp.float32
        ).astype(jnp.bfloat16)
        got = lax.all_to_all(first, "seq", split_axis=0, concat_axis=0, tiled=True)
        second = jnp.einsum(
            "ixsa,siac->xic",
            left_blocks[start : start + part].reshape(part, blocks, devices, rows_a),
            got,
            preferred_element_type=jnp.float32,
        ).astype(jnp.bfloat16)
        back = lax.all_to_all(
            second.reshape(devices, rows_a, part, width), "seq", split_axis=0, concat_axis=0, tiled=True
        )
        if part % 8 == 0:
            rows_step = 2 if part == 8 and rows_a % 2 == 0 else 1
            out = gate_mix(pieces, back, mix, out, start, rows_step)
        else:
            hidden = jnp.swapaxes(back, 0, 1)
            gated = (pieces.astype(jnp.float32) * hidden.astype(jnp.float32)).astype(jnp.bfloat16)
            out = jnp.dot(gated.reshape(-1, width), mix, preferred_element_type=jnp.float32).astype(
                jnp.bfloat16
            )
    return out.reshape(rows_a * block_len, width)


GROUP = 16
SPLIT = 4


def partner_orders(devices):
    half = devices // 2
    far = [half + half // 2 + k for k in range(half // 2)] + [half + k for k in range(half // 2)]
    pairs = half // 4
    far = [
        far[side * (half // 2) + 2 * pair + core] for pair in range(pairs) for side in (0, 1) for core in (0, 1)
    ]
    near = list(range(half // 2, half)) + list(range(2, half // 2)) + [1]
    return far, near


def flip(index, bits, devices):
    partner, bit = index, 1
    while bit < devices:
        if bits & bit:
            partner = partner + bit * (1 - 2 * lax.rem(lax.div(index, bit), 2))
        bit *= 2
    return partner


def turn_matrix(rows, first_row):
    r = lax.broadcasted_iota(jnp.int32, (rows, GROUP * GROUP), 0) + first_row
    c = lax.broadcasted_iota(jnp.int32, (rows, GROUP * GROUP), 1)
    return (c == lax.rem(r, GROUP) * GROUP + lax.div(r, GROUP)).astype(jnp.float32).astype(jnp.bfloat16)


def exchange(devices, halves, tokens, right, left, first_t, second_rows):
    tile = GROUP * GROUP
    width = tokens.shape[-1]
    cols = width // SPLIT
    chunks = halves * SPLIT
    part = GROUP // SPLIT
    rows_back = part * GROUP
    block_len = right.shape[-1]
    steps = chunks * GROUP
    groups = devices // SPLIT
    far, near = partner_orders(devices)
    x_depth = 4

    def kernel(
        x_ref, tok_ref, right_ref, left_ref, first_ref, second_ref,
        m_ref, recv_ref, back_ref, mix_out,
        buf, mix, work, xs, ws, lefts, hid, gated, mout, turn,
        fwd_send, fwd_recv, bwd_send, bwd_recv, x_sem, w_sem, l_sem, t_sem, h_sem, o_sem, own_sem, mix_sem,
    ):
        me = lax.axis_index("seq")
        to = {k: flip(me, k, devices) for k in range(1, devices)}

        def x_copy(i):
            t, a, slot = lax.div(i, GROUP), lax.rem(i, GROUP), lax.rem(i, x_depth)
            col = pl.multiple_of(lax.rem(t, SPLIT) * cols, cols)
            return pltpu.make_async_copy(
                x_ref.at[a, :, :, pl.ds(col, cols)], xs.at[pl.ds(slot * 2, 2)], x_sem.at[slot]
            )

        def w_copy(i):
            t, a, slot = lax.div(i, GROUP), lax.rem(i, GROUP), lax.rem(i, x_depth)
            row = pl.multiple_of(lax.div(t, SPLIT) * GROUP, GROUP)
            return pltpu.make_async_copy(
                right_ref.at[a, :, pl.ds(row, GROUP), :], ws.at[slot], w_sem.at[slot]
            )

        for i in range(x_depth - 1):
            x_copy(i).start()
            w_copy(i).start()

        barrier = pltpu.get_barrier_semaphore()
        for k in range(1, devices):
            pl.semaphore_signal(barrier, inc=1, device_id={"seq": to[k]}, device_id_type=pl.DeviceIdType.MESH)
        turn[...] = turn_matrix(tile, 0)
        pl.semaphore_wait(barrier, devices - 1)

        def fwd(t, k):
            return pltpu.make_async_remote_copy(
                src_ref=buf.at[t, to[k]],
                dst_ref=recv_ref.at[t, me],
                send_sem=fwd_send.at[t, k],
                recv_sem=fwd_recv.at[t, k],
                device_id={"seq": to[k]},
                device_id_type=pl.DeviceIdType.MESH,
            )

        def bwd(q, k):
            return pltpu.make_async_remote_copy(
                src_ref=buf.at[q, to[k]],
                dst_ref=back_ref.at[q, me],
                send_sem=bwd_send.at[q, k],
                recv_sem=bwd_recv.at[q, k],
                device_id={"seq": to[k]},
                device_id_type=pl.DeviceIdType.MESH,
            )

        def own_fwd(t):
            return pltpu.make_async_copy(buf.at[t, me], recv_ref.at[t, me], own_sem.at[0, t])

        def own_bwd(q):
            return pltpu.make_async_copy(buf.at[q, me], back_ref.at[q, me], own_sem.at[1, q])

        @pl.loop(0, chunks)
        def _(t):
            @pl.loop(0, GROUP)
            def _(a):
                i = t * GROUP + a
                x_copy(i).wait()
                w_copy(i).wait()

                @pl.when(i + x_depth - 1 < steps)
                def _():
                    x_copy(i + x_depth - 1).start()
                    w_copy(i + x_depth - 1).start()

                slot = lax.rem(i, x_depth)
                w = ws[slot].reshape(tile, block_len)
                x = xs[pl.ds(slot * 2, 2)].reshape(block_len, cols)
                res = jnp.dot(w, x, preferred_element_type=jnp.float32).astype(jnp.bfloat16)
                work[a] = res.reshape(devices, GROUP, cols)

            @pl.loop(0, devices)
            def _(d):
                v = work[pl.ds(0, GROUP), d].reshape(tile, cols)
                buf[t, d] = jnp.dot(turn[...], v, preferred_element_type=jnp.float32).astype(jnp.bfloat16)

            for k in far:
                fwd(t, k).start()
            own_fwd(t).start()

        @pl.loop(0, chunks)
        def _(t):
            for k in near:
                fwd(t, k).start()

        reps = width // first_ref.shape[-1]

        @pl.loop(0, first_ref.shape[0])
        def _(k):
            rows = first_ref.shape[1]
            f = first_ref[k].astype(jnp.float32)
            s = second_ref[k].astype(jnp.float32)
            full = jnp.concatenate([f] * reps, axis=1) * s
            mix[pl.ds(pl.multiple_of(k * rows, rows), rows), :] = full.astype(jnp.bfloat16)

        mix_copy = pltpu.make_async_copy(mix, mix_out, mix_sem.at[0])
        mix_copy.start()

        def f_copy(b):
            h, row = lax.div(b, GROUP), pl.multiple_of(lax.rem(b, GROUP) * GROUP, GROUP)
            slot = lax.rem(b, 2)
            return pltpu.make_async_copy(
                recv_ref.at[pl.ds(h * SPLIT, SPLIT), :, pl.ds(row, GROUP), :],
                work.at[pl.ds(slot * SPLIT, SPLIT)],
                x_sem.at[slot],
            )

        def l_copy(b):
            slot = lax.rem(b, 2)
            return pltpu.make_async_copy(left_ref.at[b], lefts.at[slot], l_sem.at[slot])

        @pl.loop(0, halves)
        def _(h):
            @pl.loop(h * SPLIT, (h + 1) * SPLIT)
            def _(t):
                own_fwd(t).wait()
                for k in far + near:
                    fwd(t, k).wait_recv()

            f_copy(h * GROUP).start()
            l_copy(h * GROUP).start()

            @pl.loop(0, SPLIT)
            def _(s):
                q = h * SPLIT + s
                for k in far + near:
                    fwd(q, k).wait_send()

                @pl.loop(0, part)
                def _(p):
                    i = s * part + p
                    b = h * GROUP + i
                    slot = lax.rem(b, 2)
                    f_copy(b).wait()
                    l_copy(b).wait()

                    @pl.when(i + 1 < GROUP)
                    def _():
                        f_copy(b + 1).start()
                        l_copy(b + 1).start()

                    for c in range(SPLIT):
                        v = work[slot * SPLIT + c].reshape(tile, cols)
                        res = jnp.dot(lefts[slot], v, preferred_element_type=jnp.float32).astype(jnp.bfloat16)
                        row = pl.multiple_of(c * rows_back + p * GROUP, GROUP)
                        buf[q, :, pl.ds(row, GROUP), :] = res.reshape(devices, GROUP, cols)

                for k in far + near:
                    bwd(q, k).start()
                own_bwd(q).start()

        def t_copies(i, slot):
            q, g = lax.div(i, groups), lax.rem(i, groups)
            row = pl.multiple_of(lax.div(q, SPLIT) * GROUP, GROUP)
            return [
                pltpu.make_async_copy(
                    tok_ref.at[:, g * SPLIT + e, pl.ds(row, GROUP), pl.ds(c * cols, cols)],
                    work.at[slot * GROUP + e * SPLIT + c],
                    t_sem.at[slot, e * SPLIT + c],
                )
                for e in range(SPLIT)
                for c in range(SPLIT)
            ]

        def h_copy(i, slot):
            q, g = lax.div(i, groups), lax.rem(i, groups)
            return pltpu.make_async_copy(back_ref.at[q, pl.ds(g * SPLIT, SPLIT)], hid.at[slot], h_sem.at[slot])

        def o_copies(i, slot):
            q, g = lax.div(i, groups), lax.rem(i, groups)
            h, s = lax.div(q, SPLIT), lax.rem(q, SPLIT)
            row = pl.multiple_of(s * rows_back, rows_back)
            return [
                pltpu.make_async_copy(
                    mout.at[slot, pl.ds(e * rows_back, rows_back)],
                    m_ref.at[h, g * SPLIT + e, pl.ds(row, rows_back)],
                    o_sem.at[slot, e],
                )
                for e in range(SPLIT)
            ]

        def turned(i, slot, e, c):
            row = pl.multiple_of(lax.rem(lax.div(i, groups), SPLIT) * rows_back, rows_back)
            v = work[slot * GROUP + e * SPLIT + c].reshape(tile, cols)
            return jnp.dot(turn[pl.ds(row, rows_back)], v, preferred_element_type=jnp.float32)

        last = chunks - 1

        for i in range(groups):
            for copy in t_copies(last * groups + i, 0):
                copy.start()
            for copy in t_copies(last * groups + i, 0):
                copy.wait()
            for e in range(SPLIT):
                for c in range(SPLIT):
                    mout[0, e * rows_back : (e + 1) * rows_back, c * cols : (c + 1) * cols] = turned(
                        last * groups + i, 0, e, c
                    ).astype(jnp.bfloat16)
            for copy in o_copies(last * groups + i, 0):
                copy.start()
            for copy in o_copies(last * groups + i, 0):
                copy.wait()

        @pl.loop(0, last)
        def _(q):
            for copy in t_copies(q * groups, 0):
                copy.start()
            own_bwd(q).wait()
            for k in far + near:
                bwd(q, k).wait_recv()
            h_copy(q * groups, 0).start()

            @pl.loop(0, groups)
            def _(g):
                i = q * groups + g
                slot = lax.rem(g, 2)
                for copy in t_copies(i, slot):
                    copy.wait()
                h_copy(i, slot).wait()

                @pl.when(g + 1 < groups)
                def _():
                    for copy in t_copies(i + 1, 1 - slot):
                        copy.start()
                    h_copy(i + 1, 1 - slot).start()

                for e in range(SPLIT):
                    for c in range(SPLIT):
                        h = hid[slot, e, c * rows_back : (c + 1) * rows_back, :].astype(jnp.float32)
                        gated[e * rows_back : (e + 1) * rows_back, c * cols : (c + 1) * cols] = (
                            turned(i, slot, e, c) * h
                        ).astype(jnp.bfloat16)
                for c in range(SPLIT):
                    mout[0, :, c * cols : (c + 1) * cols] = jnp.dot(
                        gated[...], mix[:, c * cols : (c + 1) * cols], preferred_element_type=jnp.float32
                    ).astype(jnp.bfloat16)
                for copy in o_copies(i, 0):
                    copy.start()
                for copy in o_copies(i, 0):
                    copy.wait()

        own_bwd(last).wait()
        for k in far + near:
            bwd(last, k).wait_recv()
        mix_copy.wait()

        @pl.loop(0, chunks)
        def _(q):
            for k in far + near:
                bwd(q, k).wait_send()

    bf16 = jnp.bfloat16
    anywhere = pl.BlockSpec(memory_space=pl.ANY)
    vmem = pl.BlockSpec(memory_space=pltpu.VMEM)
    dma = pltpu.SemaphoreType.DMA
    return pl.pallas_call(
        kernel,
        out_shape=(
            jax.ShapeDtypeStruct((halves, devices, tile, width), bf16),
            jax.ShapeDtypeStruct((chunks, devices, tile, cols), bf16),
            jax.ShapeDtypeStruct((chunks, devices, tile, cols), bf16),
            jax.ShapeDtypeStruct((width, width), bf16),
        ),
        in_specs=[anywhere] * 4 + [vmem] * 2,
        out_specs=[anywhere] * 4,
        scratch_shapes=[
            pltpu.VMEM((chunks, devices, tile, cols), bf16),
            pltpu.VMEM((width, width), bf16),
            pltpu.VMEM((2 * GROUP, GROUP, GROUP, cols), bf16),
            pltpu.VMEM((2 * x_depth, tile, cols), bf16),
            pltpu.VMEM((x_depth, devices, GROUP, block_len), bf16),
            pltpu.VMEM((2, tile, tile), bf16),
            pltpu.VMEM((2, SPLIT, tile, cols), bf16),
            pltpu.VMEM((tile, width), bf16),
            pltpu.VMEM((1, tile, width), bf16),
            pltpu.VMEM((tile, tile), bf16),
            dma((chunks, devices)),
            dma((chunks, devices)),
            dma((chunks, devices)),
            dma((chunks, devices)),
            dma((x_depth,)),
            dma((x_depth,)),
            dma((2,)),
            dma((2, SPLIT * SPLIT)),
            dma((2,)),
            dma((1, SPLIT)),
            dma((2, chunks)),
            dma((1,)),
        ],
        compiler_params=pltpu.CompilerParams(
            collective_id=0, has_side_effects=True, vmem_limit_bytes=60 * 2**20
        ),
        cost_estimate=pl.CostEstimate(flops=96 * 10**9, bytes_accessed=400 * 2**20, transcendentals=0),
        name="exchange",
    )(*tokens_views(tokens, devices), right, left, first_t, second_rows)


def tokens_views(tokens, devices):
    rows_a, width = tokens.shape[0], tokens.shape[-1]
    return tokens, tokens.reshape(rows_a, devices, -1, width)


def finish(m, back, mix):
    halves, devices, tile, width = m.shape
    cols = back.shape[-1]
    rows_back = tile // SPLIT
    groups = devices // SPLIT
    last = halves - 1

    def kernel(m_ref, back_ref, mix_ref, out_ref):
        turn = turn_matrix(tile, 0)

        def put(e, v):
            res = jnp.dot(turn, v, preferred_element_type=jnp.float32).astype(jnp.bfloat16)
            out_ref[:, e] = res.reshape(GROUP, GROUP, width)

        @pl.when(pl.program_id(0) < last)
        def _():
            for e in range(SPLIT):
                put(e, m_ref[0, e])

        @pl.when(pl.program_id(0) == last)
        def _():
            rows = []
            for e in range(SPLIT):
                h = jnp.concatenate(
                    [back_ref[0, e, c * rows_back : (c + 1) * rows_back, :] for c in range(SPLIT)], axis=1
                )
                x = m_ref[0, e, tile - rows_back :, :]
                rows.append((x.astype(jnp.float32) * h.astype(jnp.float32)).astype(jnp.bfloat16))
            res = jnp.dot(
                jnp.concatenate(rows, axis=0), mix_ref[...], preferred_element_type=jnp.float32
            ).astype(jnp.bfloat16)
            for e in range(SPLIT):
                done = m_ref[0, e, : tile - rows_back, :]
                put(e, jnp.concatenate([done, res[e * rows_back : (e + 1) * rows_back]], axis=0))

    rows_a = tile // GROUP
    return pl.pallas_call(
        kernel,
        grid=(halves, groups),
        in_specs=[
            pl.BlockSpec((1, SPLIT, tile, width), lambda h, g: (h, g, 0, 0)),
            pl.BlockSpec(
                (1, SPLIT, tile, cols), lambda h, g: (halves * SPLIT - 1, jnp.where(h == last, g, 0), 0, 0)
            ),
            pl.BlockSpec((width, width), lambda h, g: (0, 0)),
        ],
        out_specs=pl.BlockSpec((rows_a, SPLIT, GROUP, width), lambda h, g: (0, g, h, 0)),
        out_shape=jax.ShapeDtypeStruct((rows_a, devices, halves * GROUP, width), jnp.bfloat16),
        compiler_params=pltpu.CompilerParams(vmem_limit_bytes=56 * 2**20),
        name="finish",
    )(m, back, mix)


def on_device(devices, tokens, right_blocks, left_blocks, chan_first, chan_second):
    rows_a, block_len, _ = right_blocks.shape
    width = tokens.shape[1]
    own_b = left_blocks.shape[0]
    fits = (
        rows_a == GROUP
        and devices == GROUP
        and own_b == 2 * GROUP
        and left_blocks.shape[1] == GROUP * GROUP
        and block_len == 2 * GROUP * GROUP
        and width % 2048 == 0
    )
    if not fits:
        return plain_device(devices, tokens, right_blocks, left_blocks, chan_first, chan_second)
    x = tokens.reshape(rows_a, 2, GROUP * GROUP, width)
    right = right_blocks.reshape(rows_a, devices, own_b, block_len)
    first_t = jnp.concatenate([chan_first.transpose(0, 2, 1)] * 2, axis=2)
    second_rows = chan_second.transpose(2, 1, 0).reshape(chan_second.shape[2], 1, width)
    m, _, back, mix = exchange(devices, own_b // GROUP, x, right, left_blocks, first_t, second_rows)
    out = finish(m, back, mix)
    return out.reshape(rows_a * block_len, width)


def solution(mesh):
    devices = mesh.shape["seq"]

    def run(*args):
        return on_device(devices, *args)

    return jax.shard_map(
        run,
        mesh=mesh,
        in_specs=(P(("groups", "seq"), None), P("seq", None, None), P("seq", None, None), P(), P()),
        out_specs=P(("groups", "seq"), None),
        check_vma=False,
    )
```

```python
import jax
import jax.numpy as jnp
from jax import lax
from jax.experimental import pallas as pl
from jax.experimental.pallas import tpu as pltpu
from jax.sharding import PartitionSpec as P


def chunk_list(own_b):
    if own_b % 32 == 0:
        quarter = own_b // 4
        return [(0, quarter), (2 * quarter, 2 * quarter), (quarter, quarter)]
    return [(0, own_b)]


def gate_mix(tokens, hidden, mix, out, start, rows_step):
    rows_a, devices, _, width = tokens.shape
    part = hidden.shape[2]
    rows = rows_step * devices * part

    def kernel(tokens_ref, hidden_ref, mix_ref, *refs):
        out_ref = refs[-1]
        for r in range(rows_step):
            gated = tokens_ref[r].astype(jnp.float32) * hidden_ref[:, r].astype(jnp.float32)
            gated = gated.reshape(rows // rows_step, width).astype(jnp.bfloat16)
            res = jnp.dot(gated, mix_ref[...], preferred_element_type=jnp.float32)
            out_ref[r] = res.reshape(devices, part, width).astype(jnp.bfloat16)

    own = pl.BlockSpec((rows_step, devices, part, width), lambda a: (a, 0, start // part, 0))
    in_specs = [
        own,
        pl.BlockSpec((devices, rows_step, part, width), lambda a: (0, a, 0, 0)),
        pl.BlockSpec((width, width), lambda a: (0, 0)),
    ]
    operands = [tokens, hidden, mix]
    aliases = {}
    if out is not None:
        in_specs.append(pl.BlockSpec(memory_space=pl.ANY))
        operands.append(out)
        aliases = {3: 0}
    total = rows_a * devices * part
    return pl.pallas_call(
        kernel,
        grid=(rows_a // rows_step,),
        in_specs=in_specs,
        out_specs=own,
        out_shape=jax.ShapeDtypeStruct(tokens.shape, jnp.bfloat16),
        input_output_aliases=aliases,
        compiler_params=pltpu.CompilerParams(vmem_limit_bytes=56 * 2**20),
        cost_estimate=pl.CostEstimate(
            flops=2 * total * width * width,
            bytes_accessed=6 * total * width + 2 * width * width,
            transcendentals=0,
        ),
        name="gate_mix",
    )(*operands)


def plain_device(devices, tokens, right_blocks, left_blocks, chan_first, chan_second):
    rows_a, block_len, _ = right_blocks.shape
    width = tokens.shape[1]
    own_b = left_blocks.shape[0]
    blocks = left_blocks.shape[1]
    mix = (
        chan_first.transpose(0, 2, 1)[:, :, None, :].astype(jnp.float32)
        * chan_second.transpose(2, 1, 0)[:, None, :, :].astype(jnp.float32)
    ).astype(jnp.bfloat16).reshape(width, width)
    x = tokens.reshape(rows_a, block_len, width)
    right = right_blocks.reshape(rows_a, devices, own_b, block_len)
    pieces = tokens.reshape(rows_a, devices, own_b, width)
    out = None
    for start, part in chunk_list(own_b):
        first = jnp.einsum(
            "adib,abc->diac", right[:, :, start : start + part], x, preferred_element_type=jnp.float32
        ).astype(jnp.bfloat16)
        got = lax.all_to_all(first, "seq", split_axis=0, concat_axis=0, tiled=True)
        second = jnp.einsum(
            "ixsa,siac->xic",
            left_blocks[start : start + part].reshape(part, blocks, devices, rows_a),
            got,
            preferred_element_type=jnp.float32,
        ).astype(jnp.bfloat16)
        back = lax.all_to_all(
            second.reshape(devices, rows_a, part, width), "seq", split_axis=0, concat_axis=0, tiled=True
        )
        if part % 8 == 0:
            rows_step = 2 if part == 8 and rows_a % 2 == 0 else 1
            out = gate_mix(pieces, back, mix, out, start, rows_step)
        else:
            hidden = jnp.swapaxes(back, 0, 1)
            gated = (pieces.astype(jnp.float32) * hidden.astype(jnp.float32)).astype(jnp.bfloat16)
            out = jnp.dot(gated.reshape(-1, width), mix, preferred_element_type=jnp.float32).astype(
                jnp.bfloat16
            )
    return out.reshape(rows_a * block_len, width)


GROUP = 16
SPLIT = 4


def partner_orders(devices):
    half = devices // 2
    far = [half + half // 2 + k for k in range(half // 2)] + [half + k for k in range(half // 2)]
    pairs = half // 4
    far = [
        far[side * (half // 2) + 2 * pair + core] for pair in range(pairs) for side in (0, 1) for core in (0, 1)
    ]
    near = list(range(half // 2, half)) + list(range(2, half // 2)) + [1]
    return far, near


def flip(index, bits, devices):
    partner, bit = index, 1
    while bit < devices:
        if bits & bit:
            partner = partner + bit * (1 - 2 * lax.rem(lax.div(index, bit), 2))
        bit *= 2
    return partner


def turn_matrix(rows, first_row):
    r = lax.broadcasted_iota(jnp.int32, (rows, GROUP * GROUP), 0) + first_row
    c = lax.broadcasted_iota(jnp.int32, (rows, GROUP * GROUP), 1)
    return (c == lax.rem(r, GROUP) * GROUP + lax.div(r, GROUP)).astype(jnp.float32).astype(jnp.bfloat16)


def exchange(devices, halves, tokens, right, left, chan_first, chan_second):
    tile = GROUP * GROUP
    width = tokens.shape[-1]
    cols = width // SPLIT
    chunks = halves * SPLIT
    part = GROUP // SPLIT
    rows = part * GROUP
    block_len = right.shape[-1]
    steps = chunks * GROUP
    groups = devices // SPLIT
    far, near = partner_orders(devices)
    order = far + near
    x_depth = 4
    lag = 3
    last = chunks - 1
    early = (halves - 1) * SPLIT
    heads, head = chan_first.shape[0], chan_first.shape[1]
    bf16, f32 = jnp.bfloat16, jnp.float32

    def kernel(
        x_ref, tok_ref, right_ref, left_ref, first_ref, second_ref,
        last_ref, extra_ref, recv_ref, back_ref, mix, buf,
        work, xs, ws, lefts, hid, gated, turn, firsts, seconds, scale,
        fwd_send, fwd_recv, bwd_send, bwd_recv, x_sem, w_sem, l_sem, t_sem, h_sem, own_sem, mix_sem,
    ):
        me = lax.axis_index("seq")
        to = {k: flip(me, k, devices) for k in range(1, devices)}

        def x_copy(i):
            t, a, slot = lax.div(i, GROUP), lax.rem(i, GROUP), lax.rem(i, x_depth)
            col = pl.multiple_of(lax.rem(t, SPLIT) * cols, cols)
            return pltpu.make_async_copy(
                x_ref.at[a, :, :, pl.ds(col, cols)], xs.at[pl.ds(slot * 2, 2)], x_sem.at[slot]
            )

        def w_copy(i):
            t, a, slot = lax.div(i, GROUP), lax.rem(i, GROUP), lax.rem(i, x_depth)
            row = pl.multiple_of(lax.div(t, SPLIT) * GROUP, GROUP)
            return pltpu.make_async_copy(
                right_ref.at[a, :, pl.ds(row, GROUP), :], ws.at[slot], w_sem.at[slot]
            )

        for i in range(x_depth - 1):
            x_copy(i).start()
            w_copy(i).start()
        first_copy = pltpu.make_async_copy(first_ref, firsts, mix_sem.at[0])
        second_copy = pltpu.make_async_copy(second_ref, seconds, mix_sem.at[1])

        barrier = pltpu.get_barrier_semaphore()
        for k in range(1, devices):
            pl.semaphore_signal(barrier, inc=1, device_id={"seq": to[k]}, device_id_type=pl.DeviceIdType.MESH)
        turn[...] = turn_matrix(tile, 0)
        pl.semaphore_wait(barrier, devices - 1)

        def send(src, dst, k, send_sem, recv_sem):
            return pltpu.make_async_remote_copy(
                src_ref=src,
                dst_ref=dst,
                send_sem=send_sem,
                recv_sem=recv_sem,
                device_id={"seq": to[k]},
                device_id_type=pl.DeviceIdType.MESH,
            )

        def fwd_head(k):
            return send(
                buf.at[pl.ds(0, SPLIT), to[k], 0],
                recv_ref.at[pl.ds(0, SPLIT), me, 0],
                k, fwd_send.at[chunks, k], fwd_recv.at[chunks, k],
            )

        def fwd(h, q, k):
            if h == 0:
                src = buf.at[q, to[k], pl.ds(1, SPLIT - 1)]
                dst = recv_ref.at[q, me, pl.ds(1, SPLIT - 1)]
            else:
                src, dst = buf.at[q, to[k]], recv_ref.at[q, me]
            return send(src, dst, k, fwd_send.at[q, k], fwd_recv.at[q, k])

        def bwd(q, k):
            return send(buf.at[q, to[k]], back_ref.at[q, me], k, bwd_send.at[q, k], bwd_recv.at[q, k])

        def own_fwd(t):
            h, c = lax.div(t, SPLIT), lax.rem(t, SPLIT)
            return pltpu.make_async_copy(
                buf.at[pl.ds(h * SPLIT, SPLIT), me, c], recv_ref.at[pl.ds(h * SPLIT, SPLIT), me, c], own_sem.at[0, t]
            )

        def own_bwd(q):
            return pltpu.make_async_copy(buf.at[q, me], back_ref.at[q, me], own_sem.at[1, q])

        def first_slice(t):
            @pl.loop(0, GROUP)
            def _(a):
                i = t * GROUP + a
                x_copy(i).wait()
                w_copy(i).wait()

                @pl.when(i + x_depth - 1 < steps)
                def _():
                    x_copy(i + x_depth - 1).start()
                    w_copy(i + x_depth - 1).start()

                slot = lax.rem(i, x_depth)
                w = ws[slot].reshape(tile, block_len)
                x = xs[pl.ds(slot * 2, 2)].reshape(block_len, cols)
                res = jnp.dot(w, x, preferred_element_type=f32).astype(bf16)
                work[a] = res.reshape(devices, GROUP, cols)

            h, c = lax.div(t, SPLIT), lax.rem(t, SPLIT)

            @pl.loop(0, devices)
            def _(d):
                v = work[pl.ds(0, GROUP), d].reshape(tile, cols)
                res = jnp.dot(turn[...], v, preferred_element_type=f32).astype(bf16)
                buf[pl.ds(h * SPLIT, SPLIT), d, c] = res.reshape(SPLIT, part, GROUP, cols)

            own_fwd(t).start()

        first_slice(jnp.int32(0))
        for k in order:
            fwd_head(k).start()
        for h in range(halves):
            @pl.loop(1 if h == 0 else h * SPLIT, (h + 1) * SPLIT)
            def _(t):
                first_slice(t)

            @pl.loop(h * SPLIT, (h + 1) * SPLIT)
            def _(q):
                for k in order:
                    fwd(h, q, k).start()

        first_copy.start()
        second_copy.start()
        first_copy.wait()
        second_copy.wait()

        for c in range(SPLIT):
            wide = cols // head
            scale[...] = jnp.concatenate([seconds[c * wide + o] for o in range(wide)], axis=1).astype(f32)
            m = lax.broadcasted_iota(jnp.int32, (head, cols), 0)
            v = lax.broadcasted_iota(jnp.int32, (head, cols), 1)
            spread = (m == lax.rem(v, head)).astype(f32).astype(bf16)

            @pl.loop(0, heads)
            def _(k):
                f = lax.dot_general(
                    firsts[k], spread, (((0,), (0,)), ((), ())), preferred_element_type=f32
                )
                row = pl.multiple_of(k * head, head)
                mix[pl.ds(row, head), c * cols : (c + 1) * cols] = (f * scale[pl.ds(k, 1), :]).astype(bf16)

        def f_copies(q, p, slot):
            return [
                pltpu.make_async_copy(
                    recv_ref.at[q, :, c, p],
                    work.at[slot * SPLIT + c],
                    t_sem.at[slot, c],
                )
                for c in range(SPLIT)
            ]

        def l_copy(q, p, slot):
            return pltpu.make_async_copy(left_ref.at[q * part + p], lefts.at[slot], l_sem.at[slot])

        def second(h, q):
            for k in order:
                fwd(h, q, k).wait_recv()
            for copy in f_copies(q, 0, 0):
                copy.start()
            l_copy(q, 0, 0).start()
            for k in order:
                fwd(h, q, k).wait_send()

            @pl.loop(0, part)
            def _(p):
                slot = lax.rem(p, 2)
                for copy in f_copies(q, p, slot):
                    copy.wait()
                l_copy(q, p, slot).wait()

                @pl.when(p + 1 < part)
                def _():
                    for copy in f_copies(q, p + 1, 1 - slot):
                        copy.start()
                    l_copy(q, p + 1, 1 - slot).start()

                for c in range(SPLIT):
                    v = work[slot * SPLIT + c].reshape(tile, cols)
                    res = jnp.dot(lefts[slot], v, preferred_element_type=f32).astype(bf16)
                    buf[q, :, c, p] = res.reshape(devices, GROUP, cols)

            for k in order:
                bwd(q, k).start()
            own_bwd(q).start()

        def t_copies(q, g, slot):
            row = pl.multiple_of(lax.div(q, SPLIT) * GROUP, GROUP)
            return [
                pltpu.make_async_copy(
                    tok_ref.at[:, g * SPLIT + e, pl.ds(row, GROUP), pl.ds(c * cols, cols)],
                    work.at[slot * GROUP + e * SPLIT + c],
                    t_sem.at[slot, e * SPLIT + c],
                )
                for e in range(SPLIT)
                for c in range(SPLIT)
            ]

        def h_copy(q, g, slot):
            return pltpu.make_async_copy(back_ref.at[q, pl.ds(g * SPLIT, SPLIT)], hid.at[slot], h_sem.at[slot])

        def turned(q, slot, e, c):
            row = pl.multiple_of(lax.rem(q, SPLIT) * rows, rows)
            v = work[slot * GROUP + e * SPLIT + c].reshape(tile, cols)
            return jnp.dot(turn[pl.ds(row, rows)], v, preferred_element_type=f32)

        def mix_group(q, slot, put):
            for e in range(SPLIT):
                for c in range(SPLIT):
                    gated[e * rows : (e + 1) * rows, c * cols : (c + 1) * cols] = (
                        turned(q, slot, e, c) * hid[slot, e, c].reshape(rows, cols).astype(f32)
                    ).astype(bf16)
            for c in range(SPLIT):
                put(
                    c,
                    jnp.dot(
                        gated[...], mix[:, c * cols : (c + 1) * cols], preferred_element_type=f32
                    ).astype(bf16),
                )

        def gate(q):
            for copy in t_copies(q, 0, 0):
                copy.start()
            own_bwd(q).wait()
            for k in order:
                bwd(q, k).wait_recv()
            h_copy(q, 0, 0).start()
            for k in order:
                bwd(q, k).wait_send()

            @pl.loop(0, groups)
            def _(g):
                slot = lax.rem(g, 2)
                for copy in t_copies(q, g, slot):
                    copy.wait()
                h_copy(q, g, slot).wait()

                @pl.when(g + 1 < groups)
                def _():
                    for copy in t_copies(q, g + 1, 1 - slot):
                        copy.start()
                    h_copy(q, g + 1, 1 - slot).start()

                def put(c, res):
                    buf[q, pl.ds(g * SPLIT, SPLIT), c] = res.reshape(SPLIT, part, GROUP, cols)

                mix_group(q, slot, put)

        def gate_near():
            own_bwd(last).wait()
            for k in near:
                bwd(last, k).wait_recv()

            @pl.loop(0, groups // 2)
            def _(i):
                g = lax.div(me, devices // 2) * (groups // 2) + i
                h_copy(last, g, 0).start()
                for copy in t_copies(last, g, 0):
                    copy.start()
                for copy in t_copies(last, g, 0):
                    copy.wait()
                h_copy(last, g, 0).wait()

                def put(c, res):
                    work[GROUP + c] = res.reshape(GROUP, GROUP, cols)

                mix_group(last, 0, put)
                for e in range(SPLIT):
                    d = g * SPLIT + e
                    for c in range(SPLIT):
                        v = jnp.concatenate(
                            [
                                buf[early:last, d, c].reshape(tile - rows, cols),
                                work[GROUP + c, e * part : (e + 1) * part].reshape(rows, cols),
                            ],
                            axis=0,
                        )
                        res = jnp.dot(turn[...], v, preferred_element_type=f32).astype(bf16)
                        buf[early:last, d, c] = res[: tile - rows].reshape(SPLIT - 1, part, GROUP, cols)
                        hid[1, e, c] = res[tile - rows :].reshape(part, GROUP, cols)
                copy = pltpu.make_async_copy(hid.at[1], extra_ref.at[pl.ds(i * SPLIT, SPLIT)], h_sem.at[1])
                copy.start()
                copy.wait()

        @pl.loop(0, groups)
        def _(g):
            for copy in t_copies(last, g, 0):
                copy.start()
            for copy in t_copies(last, g, 0):
                copy.wait()
            for e in range(SPLIT):
                for c in range(SPLIT):
                    gated[e * rows : (e + 1) * rows, c * cols : (c + 1) * cols] = turned(last, 0, e, c).astype(bf16)
            row = pl.multiple_of(g * SPLIT * rows, SPLIT * rows)
            copy = pltpu.make_async_copy(gated, last_ref.at[pl.ds(row, SPLIT * rows)], mix_sem.at[0])
            copy.start()
            copy.wait()

        for k in order:
            fwd_head(k).wait_recv()
        for k in order:
            fwd_head(k).wait_send()

        @pl.loop(0, chunks)
        def _(t):
            own_fwd(t).wait()

        @pl.loop(0, lag)
        def _(q):
            second(0, q)

        for h in range(halves):
            @pl.loop(lag if h == 0 else h * SPLIT, (h + 1) * SPLIT)
            def _(q):
                second(h, q)
                gate(q - lag)

        for half in range(halves - 1):
            @pl.loop(0, devices)
            def _(d):
                for c in range(SPLIT):
                    v = buf[half * SPLIT : (half + 1) * SPLIT, d, c].reshape(tile, cols)
                    res = jnp.dot(turn[...], v, preferred_element_type=f32).astype(bf16)
                    buf[half * SPLIT : (half + 1) * SPLIT, d, c] = res.reshape(SPLIT, part, GROUP, cols)

        @pl.loop(chunks - lag, last)
        def _(q):
            gate(q)

        gate_near()
        for k in far:
            bwd(last, k).wait_recv()
        for k in order:
            bwd(last, k).wait_send()

    anywhere = pl.BlockSpec(memory_space=pl.ANY)
    dma = pltpu.SemaphoreType.DMA
    travel = (chunks, devices, SPLIT, part, GROUP, cols)
    return pl.pallas_call(
        kernel,
        out_shape=(
            jax.ShapeDtypeStruct((devices * rows, width), bf16),
            jax.ShapeDtypeStruct((devices // 2, SPLIT, part, GROUP, cols), bf16),
            jax.ShapeDtypeStruct(travel, bf16),
            jax.ShapeDtypeStruct(travel, bf16),
            pltpu.VMEM((width, width), bf16),
            pltpu.VMEM(travel, bf16),
        ),
        in_specs=[anywhere] * 6,
        out_specs=[anywhere] * 4 + [pl.BlockSpec(memory_space=pltpu.VMEM)] * 2,
        scratch_shapes=[
            pltpu.VMEM((2 * GROUP, GROUP, GROUP, cols), bf16),
            pltpu.VMEM((2 * x_depth, tile, cols), bf16),
            pltpu.VMEM((x_depth, devices, GROUP, block_len), bf16),
            pltpu.VMEM((2, tile, tile), bf16),
            pltpu.VMEM((2, SPLIT, SPLIT, part, GROUP, cols), bf16),
            pltpu.VMEM((tile, width), bf16),
            pltpu.VMEM((tile, tile), bf16),
            pltpu.VMEM(chan_first.shape, bf16),
            pltpu.VMEM((heads, heads, head), bf16),
            pltpu.VMEM((heads, cols), f32),
            dma((chunks + 1, devices)),
            dma((chunks + 1, devices)),
            dma((chunks, devices)),
            dma((chunks, devices)),
            dma((x_depth,)),
            dma((x_depth,)),
            dma((2,)),
            dma((2, SPLIT * SPLIT)),
            dma((2,)),
            dma((2, chunks)),
            dma((2,)),
        ],
        compiler_params=pltpu.CompilerParams(
            collective_id=0, has_side_effects=True, vmem_limit_bytes=19 * 2**20
        ),
        cost_estimate=pl.CostEstimate(flops=96 * 10**9, bytes_accessed=400 * 2**20, transcendentals=0),
        name="exchange",
    )(*token_views(tokens, devices), right, left, chan_first, chan_second.transpose(1, 2, 0))


def token_views(tokens, devices):
    rows_a, width = tokens.shape[0], tokens.shape[-1]
    return tokens, tokens.reshape(rows_a, devices, -1, width)


def finish(x_last, extra, back, mix, buf):
    chunks, devices, _, part, _, cols = back.shape
    rows = part * GROUP
    tile = GROUP * GROUP
    width = mix.shape[0]
    halves = chunks // SPLIT
    last = chunks - 1
    early = (halves - 1) * SPLIT
    half = devices // 2
    ahead = 4
    f32, bf16 = jnp.float32, jnp.bfloat16

    def kernel(
        x_ref, extra_ref, back_ref, mix_ref, buf_ref, out_ref,
        xs, hid, ext, gated, res, stage, turn, x_sem, h_sem, m_sem, o_sem, n_sem, e_sem, s_sem,
    ):
        side = lax.div(lax.axis_index("seq"), half)
        near, far = side * half, (1 - side) * half
        late = pl.ds((halves - 1) * GROUP, GROUP)

        def in_copies(j):
            d = far + j
            row, to = pl.multiple_of(d * rows, rows), pl.multiple_of(j * rows, rows)
            return [
                pltpu.make_async_copy(back_ref.at[last, d], hid.at[j], h_sem.at[j]),
                pltpu.make_async_copy(x_ref.at[pl.ds(row, rows)], xs.at[pl.ds(to, rows)], x_sem.at[j]),
                pltpu.make_async_copy(extra_ref.at[j], ext.at[j], m_sem.at[j]),
            ]

        def whole_copies(h, d):
            return [
                pltpu.make_async_copy(
                    buf_ref.at[pl.ds(h * SPLIT, SPLIT), d, c],
                    out_ref.at[:, :, d, pl.ds(h * GROUP, GROUP), pl.ds(c * cols, cols)],
                    o_sem.at[h, d, c],
                )
                for c in range(SPLIT)
            ]

        def near_copies(j):
            d = near + j
            return [
                copy
                for c in range(SPLIT)
                for copy in (
                    pltpu.make_async_copy(
                        buf_ref.at[pl.ds(early, SPLIT - 1), d, c],
                        out_ref.at[pl.ds(0, SPLIT - 1), :, d, late, pl.ds(c * cols, cols)],
                        n_sem.at[j, c],
                    ),
                    pltpu.make_async_copy(
                        ext.at[j, c],
                        out_ref.at[SPLIT - 1, :, d, late, pl.ds(c * cols, cols)],
                        e_sem.at[j, c],
                    ),
                )
            ]

        def tail(j, c, slot):
            return pltpu.make_async_copy(
                stage.at[slot], out_ref.at[:, :, far + j, late, pl.ds(c * cols, cols)], s_sem.at[slot]
            )

        @pl.loop(0, half)
        def _(j):
            for copy in in_copies(j):
                copy.start()

        @pl.loop(0, ahead)
        def _(d):
            for copy in whole_copies(0, d):
                copy.start()

        turn[...] = turn_matrix(tile, 0)

        @pl.loop(0, half)
        def _(j):
            for copy in in_copies(j):
                copy.wait()
            row = pl.multiple_of(j * rows, rows)
            for c in range(SPLIT):
                x = xs[pl.ds(row, rows), c * cols : (c + 1) * cols].astype(f32)
                gated[pl.ds(row, rows), c * cols : (c + 1) * cols] = (
                    x * hid[j, c].reshape(rows, cols).astype(f32)
                ).astype(bf16)

        for h in range(halves - 1):
            @pl.loop(ahead if h == 0 else 0, devices)
            def _(d):
                for copy in whole_copies(h, d):
                    copy.start()

        @pl.loop(0, half)
        def _(j):
            for copy in near_copies(j):
                copy.start()

        for c in range(SPLIT):
            res[...] = jnp.dot(
                gated[...], mix_ref[:, c * cols : (c + 1) * cols], preferred_element_type=f32
            ).astype(bf16)

            @pl.loop(0, half)
            def _(j):
                if c > 0:
                    tail(j, c - 1, j).wait()
                row = pl.multiple_of(j * rows, rows)
                v = jnp.concatenate(
                    [buf_ref[early:last, far + j, c].reshape(tile - rows, cols), res[pl.ds(row, rows)]], axis=0
                )
                out = jnp.dot(turn[...], v, preferred_element_type=f32).astype(bf16)
                stage[j] = out.reshape(SPLIT, part, GROUP, cols)
                tail(j, c, j).start()

        for h in range(halves - 1):
            @pl.loop(0, devices)
            def _(d):
                for copy in whole_copies(h, d):
                    copy.wait()

        @pl.loop(0, half)
        def _(j):
            for copy in near_copies(j):
                copy.wait()
            tail(j, SPLIT - 1, j).wait()

    anywhere = pl.BlockSpec(memory_space=pl.ANY)
    vmem = pl.BlockSpec(memory_space=pltpu.VMEM)
    dma = pltpu.SemaphoreType.DMA
    return pl.pallas_call(
        kernel,
        in_specs=[anywhere, anywhere, anywhere, vmem, vmem],
        out_specs=anywhere,
        out_shape=jax.ShapeDtypeStruct((SPLIT, part, devices, halves * GROUP, width), bf16),
        scratch_shapes=[
            pltpu.VMEM((half * rows, width), bf16),
            pltpu.VMEM((half, SPLIT, part, GROUP, cols), bf16),
            pltpu.VMEM((half, SPLIT, part, GROUP, cols), bf16),
            pltpu.VMEM((half * rows, width), bf16),
            pltpu.VMEM((half * rows, cols), bf16),
            pltpu.VMEM((half, SPLIT, part, GROUP, cols), bf16),
            pltpu.VMEM((tile, tile), bf16),
            dma((half,)),
            dma((half,)),
            dma((half,)),
            dma((max(halves - 1, 1), devices, SPLIT)),
            dma((half, SPLIT)),
            dma((half, SPLIT)),
            dma((half,)),
        ],
        compiler_params=pltpu.CompilerParams(vmem_limit_bytes=14 * 2**20),
        name="finish",
    )(x_last, extra, back, *(pltpu.with_memory_space_constraint(v, pltpu.VMEM) for v in (mix, buf)))


def on_device(devices, tokens, right_blocks, left_blocks, chan_first, chan_second):
    rows_a, block_len, _ = right_blocks.shape
    width = tokens.shape[1]
    own_b = left_blocks.shape[0]
    fits = (
        rows_a == GROUP
        and devices == GROUP
        and own_b == 2 * GROUP
        and left_blocks.shape[1] == GROUP * GROUP
        and block_len == 2 * GROUP * GROUP
        and width % 2048 == 0
    )
    if not fits:
        return plain_device(devices, tokens, right_blocks, left_blocks, chan_first, chan_second)
    x = tokens.reshape(rows_a, 2, GROUP * GROUP, width)
    right = right_blocks.reshape(rows_a, devices, own_b, block_len)
    x_last, extra, _, back, mix, buf = exchange(
        devices, own_b // GROUP, x, right, left_blocks, chan_first, chan_second
    )
    out = finish(x_last, extra, back, mix, buf)
    return out.reshape(rows_a * block_len, width)


def solution(mesh):
    devices = mesh.shape["seq"]

    def run(*args):
        return on_device(devices, *args)

    return jax.shard_map(
        run,
        mesh=mesh,
        in_specs=(P(("groups", "seq"), None), P("seq", None, None), P("seq", None, None), P(), P()),
        out_specs=P(("groups", "seq"), None),
        check_vma=False,
    )
```

```python
import jax
import jax.numpy as jnp
from jax import lax
from jax.experimental import pallas as pl
from jax.experimental.pallas import tpu as pltpu
from jax.sharding import PartitionSpec as P


def chunk_list(own_b):
    if own_b % 32 == 0:
        quarter = own_b // 4
        return [(0, quarter), (2 * quarter, 2 * quarter), (quarter, quarter)]
    return [(0, own_b)]


def gate_mix(tokens, hidden, mix, out, start, rows_step):
    rows_a, devices, _, width = tokens.shape
    part = hidden.shape[2]
    rows = rows_step * devices * part

    def kernel(tokens_ref, hidden_ref, mix_ref, *refs):
        out_ref = refs[-1]
        for r in range(rows_step):
            gated = tokens_ref[r].astype(jnp.float32) * hidden_ref[:, r].astype(jnp.float32)
            gated = gated.reshape(rows // rows_step, width).astype(jnp.bfloat16)
            res = jnp.dot(gated, mix_ref[...], preferred_element_type=jnp.float32)
            out_ref[r] = res.reshape(devices, part, width).astype(jnp.bfloat16)

    own = pl.BlockSpec((rows_step, devices, part, width), lambda a: (a, 0, start // part, 0))
    in_specs = [
        own,
        pl.BlockSpec((devices, rows_step, part, width), lambda a: (0, a, 0, 0)),
        pl.BlockSpec((width, width), lambda a: (0, 0)),
    ]
    operands = [tokens, hidden, mix]
    aliases = {}
    if out is not None:
        in_specs.append(pl.BlockSpec(memory_space=pl.ANY))
        operands.append(out)
        aliases = {3: 0}
    total = rows_a * devices * part
    return pl.pallas_call(
        kernel,
        grid=(rows_a // rows_step,),
        in_specs=in_specs,
        out_specs=own,
        out_shape=jax.ShapeDtypeStruct(tokens.shape, jnp.bfloat16),
        input_output_aliases=aliases,
        compiler_params=pltpu.CompilerParams(vmem_limit_bytes=56 * 2**20),
        cost_estimate=pl.CostEstimate(
            flops=2 * total * width * width,
            bytes_accessed=6 * total * width + 2 * width * width,
            transcendentals=0,
        ),
        name="gate_mix",
    )(*operands)


def plain_device(devices, tokens, right_blocks, left_blocks, chan_first, chan_second):
    rows_a, block_len, _ = right_blocks.shape
    width = tokens.shape[1]
    own_b = left_blocks.shape[0]
    blocks = left_blocks.shape[1]
    mix = (
        chan_first.transpose(0, 2, 1)[:, :, None, :].astype(jnp.float32)
        * chan_second.transpose(2, 1, 0)[:, None, :, :].astype(jnp.float32)
    ).astype(jnp.bfloat16).reshape(width, width)
    x = tokens.reshape(rows_a, block_len, width)
    right = right_blocks.reshape(rows_a, devices, own_b, block_len)
    pieces = tokens.reshape(rows_a, devices, own_b, width)
    out = None
    for start, part in chunk_list(own_b):
        first = jnp.einsum(
            "adib,abc->diac", right[:, :, start : start + part], x, preferred_element_type=jnp.float32
        ).astype(jnp.bfloat16)
        got = lax.all_to_all(first, "seq", split_axis=0, concat_axis=0, tiled=True)
        second = jnp.einsum(
            "ixsa,siac->xic",
            left_blocks[start : start + part].reshape(part, blocks, devices, rows_a),
            got,
            preferred_element_type=jnp.float32,
        ).astype(jnp.bfloat16)
        back = lax.all_to_all(
            second.reshape(devices, rows_a, part, width), "seq", split_axis=0, concat_axis=0, tiled=True
        )
        if part % 8 == 0:
            rows_step = 2 if part == 8 and rows_a % 2 == 0 else 1
            out = gate_mix(pieces, back, mix, out, start, rows_step)
        else:
            hidden = jnp.swapaxes(back, 0, 1)
            gated = (pieces.astype(jnp.float32) * hidden.astype(jnp.float32)).astype(jnp.bfloat16)
            out = jnp.dot(gated.reshape(-1, width), mix, preferred_element_type=jnp.float32).astype(
                jnp.bfloat16
            )
    return out.reshape(rows_a * block_len, width)


GROUP = 16
SPLIT = 4


def partner_orders(devices):
    half = devices // 2
    far = [half + half // 2 + k for k in range(half // 2)] + [half + k for k in range(half // 2)]
    pairs = half // 4
    far = [
        far[side * (half // 2) + 2 * pair + core] for pair in range(pairs) for side in (0, 1) for core in (0, 1)
    ]
    near = list(range(half // 2, half)) + list(range(2, half // 2)) + [1]
    return far, near


def flip(index, bits, devices):
    partner, bit = index, 1
    while bit < devices:
        if bits & bit:
            partner = partner + bit * (1 - 2 * lax.rem(lax.div(index, bit), 2))
        bit *= 2
    return partner


def turn_matrix(rows, first_row):
    r = lax.broadcasted_iota(jnp.int32, (rows, GROUP * GROUP), 0) + first_row
    c = lax.broadcasted_iota(jnp.int32, (rows, GROUP * GROUP), 1)
    return (c == lax.rem(r, GROUP) * GROUP + lax.div(r, GROUP)).astype(jnp.float32).astype(jnp.bfloat16)


def exchange(devices, halves, tokens, right, left, chan_first, chan_second):
    tile = GROUP * GROUP
    width = tokens.shape[-1]
    cols = width // SPLIT
    chunks = halves * SPLIT
    part = GROUP // SPLIT
    rows = part * GROUP
    block_len = right.shape[-1]
    steps = chunks * GROUP
    groups = devices // SPLIT
    far, near = partner_orders(devices)
    order = far + near
    x_depth = 4
    lag = 2
    last = chunks - 1
    early = (halves - 1) * SPLIT
    heads, head = chan_first.shape[0], chan_first.shape[1]
    bf16, f32 = jnp.bfloat16, jnp.float32

    def kernel(
        x_ref, tok_ref, right_ref, left_ref, first_ref, second_ref,
        last_ref, extra_ref, recv_ref, back_ref, mix, buf,
        work, xs, ws, lefts, hid, gated, turn, firsts, seconds, scale,
        fwd_send, fwd_recv, bwd_send, bwd_recv, x_sem, w_sem, l_sem, t_sem, h_sem, own_sem, mix_sem,
    ):
        me = lax.axis_index("seq")
        to = {k: flip(me, k, devices) for k in range(1, devices)}

        def x_copy(i):
            t, a, slot = lax.div(i, GROUP), lax.rem(i, GROUP), lax.rem(i, x_depth)
            col = pl.multiple_of(lax.rem(t, SPLIT) * cols, cols)
            return pltpu.make_async_copy(
                x_ref.at[a, :, :, pl.ds(col, cols)], xs.at[pl.ds(slot * 2, 2)], x_sem.at[slot]
            )

        def w_copy(i):
            t, a, slot = lax.div(i, GROUP), lax.rem(i, GROUP), lax.rem(i, x_depth)
            row = pl.multiple_of(lax.div(t, SPLIT) * GROUP, GROUP)
            return pltpu.make_async_copy(
                right_ref.at[a, :, pl.ds(row, GROUP), :], ws.at[slot], w_sem.at[slot]
            )

        for i in range(x_depth - 1):
            x_copy(i).start()
            w_copy(i).start()
        first_copy = pltpu.make_async_copy(first_ref, firsts, mix_sem.at[0])
        second_copy = pltpu.make_async_copy(second_ref, seconds, mix_sem.at[1])

        barrier = pltpu.get_barrier_semaphore()
        for k in range(1, devices):
            pl.semaphore_signal(barrier, inc=1, device_id={"seq": to[k]}, device_id_type=pl.DeviceIdType.MESH)
        turn[...] = turn_matrix(tile, 0)
        pl.semaphore_wait(barrier, devices - 1)

        def send(src, dst, k, send_sem, recv_sem):
            return pltpu.make_async_remote_copy(
                src_ref=src,
                dst_ref=dst,
                send_sem=send_sem,
                recv_sem=recv_sem,
                device_id={"seq": to[k]},
                device_id_type=pl.DeviceIdType.MESH,
            )

        def fwd_head(k):
            return send(
                buf.at[pl.ds(0, SPLIT), to[k], 0],
                recv_ref.at[pl.ds(0, SPLIT), me, 0],
                k, fwd_send.at[chunks, k], fwd_recv.at[chunks, k],
            )

        def fwd(h, q, k):
            if h == 0:
                src = buf.at[q, to[k], pl.ds(1, SPLIT - 1)]
                dst = recv_ref.at[q, me, pl.ds(1, SPLIT - 1)]
            else:
                src, dst = buf.at[q, to[k]], recv_ref.at[q, me]
            return send(src, dst, k, fwd_send.at[q, k], fwd_recv.at[q, k])

        def bwd(q, k):
            return send(buf.at[q, to[k]], back_ref.at[q, me], k, bwd_send.at[q, k], bwd_recv.at[q, k])

        def own_fwd(t):
            h, c = lax.div(t, SPLIT), lax.rem(t, SPLIT)
            return pltpu.make_async_copy(
                buf.at[pl.ds(h * SPLIT, SPLIT), me, c], recv_ref.at[pl.ds(h * SPLIT, SPLIT), me, c], own_sem.at[0, t]
            )

        def own_bwd(q):
            return pltpu.make_async_copy(buf.at[q, me], back_ref.at[q, me], own_sem.at[1, q])

        def first_slice(t):
            @pl.loop(0, GROUP)
            def _(a):
                i = t * GROUP + a
                x_copy(i).wait()
                w_copy(i).wait()

                @pl.when(i + x_depth - 1 < steps)
                def _():
                    x_copy(i + x_depth - 1).start()
                    w_copy(i + x_depth - 1).start()

                slot = lax.rem(i, x_depth)
                w = ws[slot].reshape(tile, block_len)
                x = xs[pl.ds(slot * 2, 2)].reshape(block_len, cols)
                res = jnp.dot(w, x, preferred_element_type=f32).astype(bf16)
                work[a] = res.reshape(devices, GROUP, cols)

            h, c = lax.div(t, SPLIT), lax.rem(t, SPLIT)

            @pl.loop(0, devices)
            def _(d):
                v = work[pl.ds(0, GROUP), d].reshape(tile, cols)
                res = jnp.dot(turn[...], v, preferred_element_type=f32).astype(bf16)
                buf[pl.ds(h * SPLIT, SPLIT), d, c] = res.reshape(SPLIT, part, GROUP, cols)

            own_fwd(t).start()

        first_slice(jnp.int32(0))
        for k in order:
            fwd_head(k).start()
        for h in range(halves):
            @pl.loop(1 if h == 0 else h * SPLIT, (h + 1) * SPLIT)
            def _(t):
                first_slice(t)

            @pl.loop(h * SPLIT, (h + 1) * SPLIT)
            def _(q):
                for k in order:
                    fwd(h, q, k).start()

        first_copy.start()
        second_copy.start()
        first_copy.wait()
        second_copy.wait()

        for c in range(SPLIT):
            wide = cols // head
            scale[...] = jnp.concatenate([seconds[c * wide + o] for o in range(wide)], axis=1).astype(f32)
            m = lax.broadcasted_iota(jnp.int32, (head, cols), 0)
            v = lax.broadcasted_iota(jnp.int32, (head, cols), 1)
            spread = (m == lax.rem(v, head)).astype(f32).astype(bf16)

            @pl.loop(0, heads)
            def _(k):
                f = lax.dot_general(
                    firsts[k], spread, (((0,), (0,)), ((), ())), preferred_element_type=f32
                )
                row = pl.multiple_of(k * head, head)
                mix[pl.ds(row, head), c * cols : (c + 1) * cols] = (f * scale[pl.ds(k, 1), :]).astype(bf16)

        def f_copies(q, p, slot):
            return [
                pltpu.make_async_copy(
                    recv_ref.at[q, :, c, p],
                    work.at[slot * SPLIT + c],
                    t_sem.at[slot, c],
                )
                for c in range(SPLIT)
            ]

        def l_copy(q, p, slot):
            return pltpu.make_async_copy(left_ref.at[q * part + p], lefts.at[slot], l_sem.at[slot])

        def second(h, q):
            for k in order:
                fwd(h, q, k).wait_recv()
            for copy in f_copies(q, 0, 0):
                copy.start()
            l_copy(q, 0, 0).start()
            for k in order:
                fwd(h, q, k).wait_send()

            @pl.loop(0, part)
            def _(p):
                slot = lax.rem(p, 2)
                for copy in f_copies(q, p, slot):
                    copy.wait()
                l_copy(q, p, slot).wait()

                @pl.when(p + 1 < part)
                def _():
                    for copy in f_copies(q, p + 1, 1 - slot):
                        copy.start()
                    l_copy(q, p + 1, 1 - slot).start()

                for c in range(SPLIT):
                    v = work[slot * SPLIT + c].reshape(tile, cols)
                    res = jnp.dot(lefts[slot], v, preferred_element_type=f32).astype(bf16)
                    buf[q, :, c, p] = res.reshape(devices, GROUP, cols)

            for k in order:
                bwd(q, k).start()
            own_bwd(q).start()

        def t_copies(q, g, slot):
            row = pl.multiple_of(lax.div(q, SPLIT) * GROUP, GROUP)
            return [
                pltpu.make_async_copy(
                    tok_ref.at[:, g * SPLIT + e, pl.ds(row, GROUP), pl.ds(c * cols, cols)],
                    work.at[slot * GROUP + e * SPLIT + c],
                    t_sem.at[slot, e * SPLIT + c],
                )
                for e in range(SPLIT)
                for c in range(SPLIT)
            ]

        def h_copy(q, g, slot):
            return pltpu.make_async_copy(back_ref.at[q, pl.ds(g * SPLIT, SPLIT)], hid.at[slot], h_sem.at[slot])

        def turned(q, slot, e, c):
            row = pl.multiple_of(lax.rem(q, SPLIT) * rows, rows)
            v = work[slot * GROUP + e * SPLIT + c].reshape(tile, cols)
            return jnp.dot(turn[pl.ds(row, rows)], v, preferred_element_type=f32)

        def mix_group(q, slot, put):
            for e in range(SPLIT):
                for c in range(SPLIT):
                    gated[e * rows : (e + 1) * rows, c * cols : (c + 1) * cols] = (
                        turned(q, slot, e, c) * hid[slot, e, c].reshape(rows, cols).astype(f32)
                    ).astype(bf16)
            for c in range(SPLIT):
                put(
                    c,
                    jnp.dot(
                        gated[...], mix[:, c * cols : (c + 1) * cols], preferred_element_type=f32
                    ).astype(bf16),
                )

        def gate(q):
            for copy in t_copies(q, 0, 0):
                copy.start()
            own_bwd(q).wait()
            for k in order:
                bwd(q, k).wait_recv()
            h_copy(q, 0, 0).start()
            for k in order:
                bwd(q, k).wait_send()

            @pl.loop(0, groups)
            def _(g):
                slot = lax.rem(g, 2)
                for copy in t_copies(q, g, slot):
                    copy.wait()
                h_copy(q, g, slot).wait()

                @pl.when(g + 1 < groups)
                def _():
                    for copy in t_copies(q, g + 1, 1 - slot):
                        copy.start()
                    h_copy(q, g + 1, 1 - slot).start()

                def put(c, res):
                    buf[q, pl.ds(g * SPLIT, SPLIT), c] = res.reshape(SPLIT, part, GROUP, cols)

                mix_group(q, slot, put)

        def gate_near():
            own_bwd(last).wait()
            for k in near:
                bwd(last, k).wait_recv()

            @pl.loop(0, groups // 2)
            def _(i):
                g = lax.div(me, devices // 2) * (groups // 2) + i
                h_copy(last, g, 0).start()
                for copy in t_copies(last, g, 0):
                    copy.start()
                for copy in t_copies(last, g, 0):
                    copy.wait()
                h_copy(last, g, 0).wait()

                def put(c, res):
                    work[GROUP + c] = res.reshape(GROUP, GROUP, cols)

                mix_group(last, 0, put)
                for e in range(SPLIT):
                    d = g * SPLIT + e
                    for c in range(SPLIT):
                        v = jnp.concatenate(
                            [
                                buf[early:last, d, c].reshape(tile - rows, cols),
                                work[GROUP + c, e * part : (e + 1) * part].reshape(rows, cols),
                            ],
                            axis=0,
                        )
                        res = jnp.dot(turn[...], v, preferred_element_type=f32).astype(bf16)
                        buf[early:last, d, c] = res[: tile - rows].reshape(SPLIT - 1, part, GROUP, cols)
                        hid[1, e, c] = res[tile - rows :].reshape(part, GROUP, cols)
                copy = pltpu.make_async_copy(hid.at[1], extra_ref.at[pl.ds(i * SPLIT, SPLIT)], h_sem.at[1])
                copy.start()
                copy.wait()

        @pl.loop(0, groups)
        def _(g):
            for copy in t_copies(last, g, 0):
                copy.start()
            for copy in t_copies(last, g, 0):
                copy.wait()
            for e in range(SPLIT):
                for c in range(SPLIT):
                    gated[e * rows : (e + 1) * rows, c * cols : (c + 1) * cols] = turned(last, 0, e, c).astype(bf16)
            row = pl.multiple_of(g * SPLIT * rows, SPLIT * rows)
            copy = pltpu.make_async_copy(gated, last_ref.at[pl.ds(row, SPLIT * rows)], mix_sem.at[0])
            copy.start()
            copy.wait()

        for k in order:
            fwd_head(k).wait_recv()
        for k in order:
            fwd_head(k).wait_send()

        @pl.loop(0, chunks)
        def _(t):
            own_fwd(t).wait()

        @pl.loop(0, lag)
        def _(q):
            second(0, q)

        for h in range(halves):
            @pl.loop(lag if h == 0 else h * SPLIT, (h + 1) * SPLIT)
            def _(q):
                second(h, q)
                gate(q - lag)

                for half in range(halves - 1):
                    @pl.when(q == (half + 1) * SPLIT - 1 + lag)
                    def _():
                        @pl.loop(0, devices)
                        def _(d):
                            for c in range(SPLIT):
                                v = buf[half * SPLIT : (half + 1) * SPLIT, d, c].reshape(tile, cols)
                                res = jnp.dot(turn[...], v, preferred_element_type=f32).astype(bf16)
                                buf[half * SPLIT : (half + 1) * SPLIT, d, c] = res.reshape(SPLIT, part, GROUP, cols)

        @pl.loop(chunks - lag, last)
        def _(q):
            gate(q)

        gate_near()
        for k in far:
            bwd(last, k).wait_recv()
        for k in order:
            bwd(last, k).wait_send()

    anywhere = pl.BlockSpec(memory_space=pl.ANY)
    dma = pltpu.SemaphoreType.DMA
    travel = (chunks, devices, SPLIT, part, GROUP, cols)
    return pl.pallas_call(
        kernel,
        out_shape=(
            jax.ShapeDtypeStruct((devices * rows, width), bf16),
            jax.ShapeDtypeStruct((devices // 2, SPLIT, part, GROUP, cols), bf16),
            jax.ShapeDtypeStruct(travel, bf16),
            jax.ShapeDtypeStruct(travel, bf16),
            pltpu.VMEM((width, width), bf16),
            pltpu.VMEM(travel, bf16),
        ),
        in_specs=[anywhere] * 6,
        out_specs=[anywhere] * 4 + [pl.BlockSpec(memory_space=pltpu.VMEM)] * 2,
        scratch_shapes=[
            pltpu.VMEM((2 * GROUP, GROUP, GROUP, cols), bf16),
            pltpu.VMEM((2 * x_depth, tile, cols), bf16),
            pltpu.VMEM((x_depth, devices, GROUP, block_len), bf16),
            pltpu.VMEM((2, tile, tile), bf16),
            pltpu.VMEM((2, SPLIT, SPLIT, part, GROUP, cols), bf16),
            pltpu.VMEM((tile, width), bf16),
            pltpu.VMEM((tile, tile), bf16),
            pltpu.VMEM(chan_first.shape, bf16),
            pltpu.VMEM((heads, heads, head), bf16),
            pltpu.VMEM((heads, cols), f32),
            dma((chunks + 1, devices)),
            dma((chunks + 1, devices)),
            dma((chunks, devices)),
            dma((chunks, devices)),
            dma((x_depth,)),
            dma((x_depth,)),
            dma((2,)),
            dma((2, SPLIT * SPLIT)),
            dma((2,)),
            dma((2, chunks)),
            dma((2,)),
        ],
        compiler_params=pltpu.CompilerParams(
            collective_id=0, has_side_effects=True, vmem_limit_bytes=19 * 2**20
        ),
        cost_estimate=pl.CostEstimate(flops=96 * 10**9, bytes_accessed=400 * 2**20, transcendentals=0),
        name="exchange",
    )(*token_views(tokens, devices), right, left, chan_first, chan_second.transpose(1, 2, 0))


def token_views(tokens, devices):
    rows_a, width = tokens.shape[0], tokens.shape[-1]
    return tokens, tokens.reshape(rows_a, devices, -1, width)


def finish(x_last, extra, back, mix, buf):
    chunks, devices, _, part, _, cols = back.shape
    rows = part * GROUP
    tile = GROUP * GROUP
    width = mix.shape[0]
    halves = chunks // SPLIT
    last = chunks - 1
    early = (halves - 1) * SPLIT
    half = devices // 2
    ahead = 4
    f32, bf16 = jnp.float32, jnp.bfloat16

    def kernel(
        x_ref, extra_ref, back_ref, mix_ref, buf_ref, out_ref,
        xs, hid, ext, gated, res, stage, turn, x_sem, h_sem, m_sem, o_sem, n_sem, e_sem, s_sem,
    ):
        side = lax.div(lax.axis_index("seq"), half)
        near, far = side * half, (1 - side) * half
        late = pl.ds((halves - 1) * GROUP, GROUP)

        def in_copies(j):
            d = far + j
            row, to = pl.multiple_of(d * rows, rows), pl.multiple_of(j * rows, rows)
            return [
                pltpu.make_async_copy(back_ref.at[last, d], hid.at[j], h_sem.at[j]),
                pltpu.make_async_copy(x_ref.at[pl.ds(row, rows)], xs.at[pl.ds(to, rows)], x_sem.at[j]),
                pltpu.make_async_copy(extra_ref.at[j], ext.at[j], m_sem.at[j]),
            ]

        def whole_copies(h, d):
            return [
                pltpu.make_async_copy(
                    buf_ref.at[pl.ds(h * SPLIT, SPLIT), d, c],
                    out_ref.at[:, :, d, pl.ds(h * GROUP, GROUP), pl.ds(c * cols, cols)],
                    o_sem.at[h, d, c],
                )
                for c in range(SPLIT)
            ]

        def near_copies(j):
            d = near + j
            return [
                copy
                for c in range(SPLIT)
                for copy in (
                    pltpu.make_async_copy(
                        buf_ref.at[pl.ds(early, SPLIT - 1), d, c],
                        out_ref.at[pl.ds(0, SPLIT - 1), :, d, late, pl.ds(c * cols, cols)],
                        n_sem.at[j, c],
                    ),
                    pltpu.make_async_copy(
                        ext.at[j, c],
                        out_ref.at[SPLIT - 1, :, d, late, pl.ds(c * cols, cols)],
                        e_sem.at[j, c],
                    ),
                )
            ]

        def tail(j, c, slot):
            return pltpu.make_async_copy(
                stage.at[slot], out_ref.at[:, :, far + j, late, pl.ds(c * cols, cols)], s_sem.at[slot]
            )

        @pl.loop(0, half)
        def _(j):
            for copy in in_copies(j):
                copy.start()

        @pl.loop(0, ahead)
        def _(d):
            for copy in whole_copies(0, d):
                copy.start()

        turn[...] = turn_matrix(tile, 0)

        @pl.loop(0, half)
        def _(j):
            for copy in in_copies(j):
                copy.wait()
            row = pl.multiple_of(j * rows, rows)
            for c in range(SPLIT):
                x = xs[pl.ds(row, rows), c * cols : (c + 1) * cols].astype(f32)
                gated[pl.ds(row, rows), c * cols : (c + 1) * cols] = (
                    x * hid[j, c].reshape(rows, cols).astype(f32)
                ).astype(bf16)

        for h in range(halves - 1):
            @pl.loop(ahead if h == 0 else 0, devices)
            def _(d):
                for copy in whole_copies(h, d):
                    copy.start()

        @pl.loop(0, half)
        def _(j):
            for copy in near_copies(j):
                copy.start()

        for c in range(SPLIT):
            res[...] = jnp.dot(
                gated[...], mix_ref[:, c * cols : (c + 1) * cols], preferred_element_type=f32
            ).astype(bf16)

            @pl.loop(0, half)
            def _(j):
                if c > 0:
                    tail(j, c - 1, j).wait()
                row = pl.multiple_of(j * rows, rows)
                v = jnp.concatenate(
                    [buf_ref[early:last, far + j, c].reshape(tile - rows, cols), res[pl.ds(row, rows)]], axis=0
                )
                out = jnp.dot(turn[...], v, preferred_element_type=f32).astype(bf16)
                stage[j] = out.reshape(SPLIT, part, GROUP, cols)
                tail(j, c, j).start()

        for h in range(halves - 1):
            @pl.loop(0, devices)
            def _(d):
                for copy in whole_copies(h, d):
                    copy.wait()

        @pl.loop(0, half)
        def _(j):
            for copy in near_copies(j):
                copy.wait()
            tail(j, SPLIT - 1, j).wait()

    anywhere = pl.BlockSpec(memory_space=pl.ANY)
    vmem = pl.BlockSpec(memory_space=pltpu.VMEM)
    dma = pltpu.SemaphoreType.DMA
    return pl.pallas_call(
        kernel,
        in_specs=[anywhere, anywhere, anywhere, vmem, vmem],
        out_specs=anywhere,
        out_shape=jax.ShapeDtypeStruct((SPLIT, part, devices, halves * GROUP, width), bf16),
        scratch_shapes=[
            pltpu.VMEM((half * rows, width), bf16),
            pltpu.VMEM((half, SPLIT, part, GROUP, cols), bf16),
            pltpu.VMEM((half, SPLIT, part, GROUP, cols), bf16),
            pltpu.VMEM((half * rows, width), bf16),
            pltpu.VMEM((half * rows, cols), bf16),
            pltpu.VMEM((half, SPLIT, part, GROUP, cols), bf16),
            pltpu.VMEM((tile, tile), bf16),
            dma((half,)),
            dma((half,)),
            dma((half,)),
            dma((max(halves - 1, 1), devices, SPLIT)),
            dma((half, SPLIT)),
            dma((half, SPLIT)),
            dma((half,)),
        ],
        compiler_params=pltpu.CompilerParams(vmem_limit_bytes=14 * 2**20),
        name="finish",
    )(x_last, extra, back, *(pltpu.with_memory_space_constraint(v, pltpu.VMEM) for v in (mix, buf)))


def on_device(devices, tokens, right_blocks, left_blocks, chan_first, chan_second):
    rows_a, block_len, _ = right_blocks.shape
    width = tokens.shape[1]
    own_b = left_blocks.shape[0]
    fits = (
        rows_a == GROUP
        and devices == GROUP
        and own_b == 2 * GROUP
        and left_blocks.shape[1] == GROUP * GROUP
        and block_len == 2 * GROUP * GROUP
        and width % 2048 == 0
    )
    if not fits:
        return plain_device(devices, tokens, right_blocks, left_blocks, chan_first, chan_second)
    x = tokens.reshape(rows_a, 2, GROUP * GROUP, width)
    right = right_blocks.reshape(rows_a, devices, own_b, block_len)
    x_last, extra, _, back, mix, buf = exchange(
        devices, own_b // GROUP, x, right, left_blocks, chan_first, chan_second
    )
    out = finish(x_last, extra, back, mix, buf)
    return out.reshape(rows_a * block_len, width)


def solution(mesh):
    devices = mesh.shape["seq"]

    def run(*args):
        return on_device(devices, *args)

    return jax.shard_map(
        run,
        mesh=mesh,
        in_specs=(P(("groups", "seq"), None), P("seq", None, None), P("seq", None, None), P(), P()),
        out_specs=P(("groups", "seq"), None),
        check_vma=False,
    )
```
